32 devices in a mesh: groups: 2 (over y), ctx: 4 (over z), head: 2 (over x), rep: 2 (over core).
Axes of the slice: x: 2, y: 2, z: 4, core: 2. Of those that a mesh axis runs over, the one named last changes fastest.
Arguments:
- queries: bfloat16 [12288, 1536], P(('groups', 'ctx', 'rep'), 'head'), parts along dimension 0, may hold values from -5 to 5
- keys_in: bfloat16 [12288, 1536], P(('groups', 'ctx', 'rep'), 'head'), parts along dimension 0, may hold values from -12 to 12
- values: bfloat16 [12288, 1536], P(('groups', 'ctx', 'rep'), 'head'), parts along dimension 0, may hold values from -6 to 6
- grad_out: bfloat16 [12288, 1536], P(('groups', 'ctx', 'rep'), 'head'), parts along dimension 0, may hold values from -6 to 6
- clip_ids: int32 [16], P('groups'), parts along dimension 0, may hold values from 0 to 2, as said below
Outputs:
- grad_query: bfloat16 [12288, 1536], P(('groups', 'ctx', 'rep'), 'head'), parts along dimension 0
- grad_key: bfloat16 [12288, 1536], P(('groups', 'ctx', 'rep'), 'head'), parts along dimension 0
- grad_value: bfloat16 [12288, 1536], P(('groups', 'ctx', 'rep'), 'head'), parts along dimension 0
The draws below stay inside these ranges and needn't reach their ends.
There are 2 independent parts, one for each index of `groups`. The reference program is written for one: setup_inputs(seed, part) draws one part's arguments, and reference() takes and returns one part's arrays. A program takes and returns all parts, laid end to end along the dimension named above; each array names one. Nothing has to cross between parts.
Inputs may be any that keep to these rules, and one draw needn't show every extreme that they name: clip_ids of the first tile row is 0, and each next tile row's id equals the previous one or exceeds it by one; a clip is the run of tile rows with one id; the last tile row's id is 2.
All inputs are finite; a program needn't handle non-finite values.
Results may differ from the reference program's by a relative error of at most 0.013.
Values may be sent and summed in bfloat16 or wider, within the bound.
A program may use at most 64 MiB of HBM per device.

```python
import math
import jax
import jax.numpy as jnp
from jax import lax

HEADS = 12
HEAD_DIM = 128
WIDTH = 1536
ROW_TOK = 768
ROWS = 8
TOKENS = 6144


def shared_pair(key):
    base_key = jax.random.fold_in(key, 11)
    first_key = jax.random.fold_in(base_key, 0)
    second_key = jax.random.fold_in(base_key, 1)
    third_key = jax.random.fold_in(base_key, 2)
    fifth_key = jax.random.fold_in(base_key, 4)
    sixth_key = jax.random.fold_in(base_key, 5)
    seventh_key = jax.random.fold_in(base_key, 6)
    shape = (TOKENS, WIDTH)
    query_vals = jnp.clip(jax.random.normal(first_key, shape, jnp.float32), -4.0, 4.0)
    key_vals = jnp.clip(jax.random.normal(second_key, shape, jnp.float32), -4.0, 4.0)
    row_scales = jnp.exp(jax.random.uniform(third_key, (TOKENS, 1), jnp.float32, math.log(0.5), math.log(1.5)))
    key_vals = key_vals * row_scales
    positions = jnp.arange(TOKENS)
    offset = jax.random.randint(fifth_key, (), 0, 53)
    paired = ((positions + offset) % 53 == 0) & (positions % ROW_TOK < ROW_TOK - 1)
    pattern = jnp.where(jax.random.normal(sixth_key, shape, jnp.float32) > 0.0, 1.0, -1.0)
    rough = jax.random.uniform(seventh_key, shape, jnp.float32, 0.7, 1.3)
    query_vals = jnp.where(paired[:, None], 2.5 * pattern, query_vals)
    partner = jnp.roll(paired, 1)
    key_vals = jnp.where(partner[:, None], 0.6 * jnp.roll(pattern, 1, axis=0) * rough, key_vals)
    return (query_vals, key_vals)


def draw_queries(key, part):
    return shared_pair(key)[0].astype(jnp.bfloat16)


def draw_keys_in(key, part):
    return shared_pair(key)[1].astype(jnp.bfloat16)


def draw_clip_ids(key, part):
    order = jax.random.permutation(jax.random.fold_in(key, 5), ROWS - 1).astype(jnp.int32) + 1
    picked = order[:2]
    fresh = jnp.zeros((ROWS,), jnp.int32).at[picked].set(1)
    return jnp.cumsum(fresh).astype(jnp.int32)


def level_of(rng, shape, cuts, least, top_value):
    level, own = 1.0, jax.random.fold_in(rng, 6)
    for position, shards_of in cuts:
        heights = jnp.exp(jax.random.uniform(jax.random.fold_in(own, position), (shards_of,), jnp.float32, least / len(cuts), top_value / len(cuts)))
        level = level * jnp.repeat(heights, shape[position] // shards_of).reshape([-1 if axis == position else 1 for axis in range(len(shape))])
    return level


def normal_values(own_key, shape, scale, limit, cuts=(), kind=jnp.bfloat16):
    drawn = jax.random.normal(own_key, shape, jnp.float32) * scale
    if len(cuts) > 0:
        drawn = level_of(own_key, shape, cuts, -0.22, 0.18) * drawn
    return jnp.clip(drawn, min=-limit, max=limit).astype(kind)


def setup_inputs(seed: int = 0, part: int = 0) -> dict:
    key_list = jax.random.split(jax.random.key(seed), 6)
    own_keys = jax.random.split(jax.random.fold_in(key_list[5], part), 6)
    return {
        "queries": draw_queries(jax.random.fold_in(jax.random.fold_in(key_list[5], part), 71), part),
        "keys_in": draw_keys_in(jax.random.fold_in(jax.random.fold_in(key_list[5], part), 71), part),
        "values": normal_values(own_keys[2], (TOKENS, WIDTH), 1.0, 6.0, ((0, 8), (1, 2))),
        "grad_out": normal_values(own_keys[3], (TOKENS, WIDTH), 1.0, 6.0, ((0, 8), (1, 2))),
        "clip_ids": draw_clip_ids(jax.random.fold_in(jax.random.fold_in(key_list[5], part), 71), part),
    }


def reference(queries, keys_in, values, grad_out, clip_ids):
    row_count = clip_ids.shape[0]
    row_tok = queries.shape[0] // row_count
    feature_width = queries.shape[1]
    softmax_scale = HEAD_DIM ** -0.5

    def by_rows(array):
        return array.reshape(row_count, row_tok, HEADS, HEAD_DIM)

    query_rows = by_rows(queries)
    grad_rows = by_rows(grad_out)
    zero_row = jnp.zeros((1, row_tok, HEADS, HEAD_DIM), jnp.bfloat16)
    key_padded = jnp.concatenate([zero_row, by_rows(keys_in), zero_row], axis=0)
    value_padded = jnp.concatenate([zero_row, by_rows(values), zero_row], axis=0)
    sentinel = jnp.full((1,), -1, jnp.int32)
    clip_padded = jnp.concatenate([sentinel, clip_ids.astype(jnp.int32), sentinel], axis=0)

    def one_row(row_index):
        query_now = query_rows[row_index].astype(jnp.float32)
        grad_now = grad_rows[row_index].astype(jnp.float32)
        key_window = lax.dynamic_slice_in_dim(key_padded, row_index, 3, 0)
        value_window = lax.dynamic_slice_in_dim(value_padded, row_index, 3, 0)
        clip_window = lax.dynamic_slice_in_dim(clip_padded, row_index, 3, 0)
        own_clip = clip_ids[row_index]
        key_mask = jnp.repeat(clip_window == own_clip, row_tok)
        key_flat = key_window.reshape(3 * row_tok, HEADS, HEAD_DIM).astype(jnp.float32)
        value_flat = value_window.reshape(3 * row_tok, HEADS, HEAD_DIM).astype(jnp.float32)
        scores = jnp.einsum("qhd,khd->hqk", query_now, key_flat) * softmax_scale
        scores = jnp.where(key_mask[None, None, :], scores, -jnp.inf)
        row_max = jnp.max(scores, axis=2, keepdims=True)
        log_total = row_max + jnp.log(jnp.sum(jnp.exp(scores - row_max), axis=2, keepdims=True))
        probs = jnp.exp(scores - log_total)
        probs_low = probs.astype(jnp.bfloat16)
        dprob = jnp.einsum("qhd,khd->hqk", grad_now, value_flat)
        row_delta = jnp.sum(probs * dprob, axis=2, keepdims=True)
        dscores = (probs * (dprob - row_delta)).astype(jnp.bfloat16)
        dscores_wide = dscores.astype(jnp.float32)
        grad_q = jnp.einsum("hqk,khd->qhd", dscores_wide, key_flat) * softmax_scale
        key_terms = jnp.einsum("hqk,qhd->khd", dscores_wide, query_now) * softmax_scale
        value_terms = jnp.einsum("hqk,qhd->khd", probs_low.astype(jnp.float32), grad_now)
        return (grad_q.astype(jnp.bfloat16).reshape(row_tok, feature_width),
                key_terms.astype(jnp.bfloat16).reshape(3, row_tok, feature_width),
                value_terms.astype(jnp.bfloat16).reshape(3, row_tok, feature_width))

    grad_q_rows, key_terms, value_terms = lax.map(one_row, jnp.arange(row_count, dtype=jnp.int32))

    def combine(block_terms):
        block_terms = block_terms.astype(jnp.float32)
        empty_row = jnp.zeros((1, row_tok, feature_width), jnp.float32)
        from_upper = jnp.concatenate([block_terms[1:, 0], empty_row], axis=0)
        from_lower = jnp.concatenate([empty_row, block_terms[:-1, 2]], axis=0)
        summed = block_terms[:, 1] + from_upper + from_lower
        return summed.astype(jnp.bfloat16).reshape(row_count * row_tok, feature_width)

    grad_query = grad_q_rows.reshape(row_count * row_tok, feature_width)
    return (grad_query, combine(key_terms), combine(value_terms))
```

```python
import math

import jax
import jax.numpy as jnp
from jax import lax
from jax.experimental import pallas as pl
from jax.experimental.pallas import tpu as pltpu
from jax.sharding import PartitionSpec as P

HEAD_DIM = 128
KEY_CHUNK = 64
QUERY_CHUNK = 256
LANES = 8
OWN_SLOTS = 4
SCALE = HEAD_DIM ** -0.5
SCALE_LOG2 = SCALE * math.log2(math.e)
MESH = pl.DeviceIdType.MESH
OWN, CORE, FAR = 0, 1, 2
LOW = jnp.bfloat16


def product(left, right, left_axis, right_axis):
    return lax.dot_general(
        left, right, (((left_axis,), (right_axis,)), ((), ())),
        preferred_element_type=jnp.float32,
    )


def attention_kernel(
    clip_ref, q_hbm, k_hbm, v_hbm, g_hbm, dq_hbm, dk_hbm, dv_hbm,
    q_all, g_all, k_all, v_all, scores, dprobs, weights, probs, dscores,
    tops, part, part_got, final, final_got, term, term_got, dq_own, total, result,
    load_sem, qg_send, qg_recv, part_send, part_recv, final_send, final_recv,
    term_send, term_recv, out_sem,
):
    heads, row_tok, _ = k_all.shape
    reps = lax.axis_size("rep")
    count = lax.axis_size("ctx") * reps
    rep = lax.axis_index("rep")
    position = lax.axis_index("ctx") * reps + rep
    core_row = position + 1 - 2 * rep
    far_row = position - 1 + 2 * rep
    has_far = (far_row >= 0) & (far_row < count)
    far_row = jnp.clip(far_row, 0, count - 1)

    def device(index):
        return {"ctx": index // reps, "rep": lax.rem(index, reps)}

    partners = (device(core_row), device(far_row))

    def each_partner(action):
        action(CORE)

        @pl.when(has_far)
        def _():
            action(FAR)

    def far_first(action):
        @pl.when(has_far)
        def _():
            action(FAR)

        action(CORE)

    def remote(source, target, send, recv, role):
        return pltpu.make_async_remote_copy(
            src_ref=source, dst_ref=target, send_sem=send, recv_sem=recv,
            device_id=partners[role - 1], device_id_type=MESH,
        )

    def q_copy(head, role):
        return remote(q_all.at[OWN, head], q_all.at[role, head],
                      qg_send.at[0, role - 1, head], qg_recv.at[0, role - 1, head], role)

    def g_copy(head, role):
        return remote(g_all.at[OWN, head], g_all.at[role, head],
                      qg_send.at[1, role - 1, head], qg_recv.at[1, role - 1, head], role)

    def part_copy(head, role):
        return remote(part.at[role, head], part_got.at[role - 1, head],
                      part_send.at[role - 1, head], part_recv.at[role - 1, head], role)

    def final_copy(head, role):
        return remote(final.at[head], final_got.at[role - 1, head],
                      final_send.at[role - 1, head], final_recv.at[role - 1, head], role)

    def term_copy(head, role):
        return remote(term.at[role - 1, head], term_got.at[role - 1, head],
                      term_send.at[role - 1, head], term_recv.at[role - 1, head], role)

    def strip(head):
        return pl.ds(pl.multiple_of(head * HEAD_DIM, HEAD_DIM), HEAD_DIM)

    def out_copy(head, which):
        target = (dq_hbm, dk_hbm, dv_hbm)[which]
        return pltpu.make_async_copy(
            result.at[which, head], target.at[:, strip(head)], out_sem.at[which, head]
        )

    def load(head, which):
        source = (q_hbm, g_hbm, k_hbm, v_hbm)[which]
        target = (q_all.at[OWN, head], g_all.at[OWN, head], k_all.at[head], v_all.at[head])[which]
        return pltpu.make_async_copy(
            source.at[:, strip(head)], target, load_sem.at[which, head]
        )

    def send_q(head):
        far_first(lambda role: q_copy(head, role).start())

    def send_g(head):
        far_first(lambda role: g_copy(head, role).start())

    barrier = pltpu.get_barrier_semaphore()
    each_partner(lambda role: pl.semaphore_signal(
        barrier, inc=1, device_id=partners[role - 1], device_id_type=MESH))
    for which in range(4):
        load(0, which).start()
    for head in range(1, heads):
        for which in range(4):
            load(head, which).start()
    pl.semaphore_wait(barrier, 1 + has_far.astype(jnp.int32))
    for head in range(heads):
        load(head, 0).wait()
        load(head, 1).wait()
        if head < 2:
            send_q(head)
            send_g(head)

    @pl.when(jnp.logical_not(has_far))
    def _():
        q_all[FAR] = jnp.zeros((heads, row_tok, HEAD_DIM), LOW)
        g_all[FAR] = jnp.zeros((heads, row_tok, HEAD_DIM), LOW)
        part_got[FAR - 1] = jnp.zeros((heads, 2, row_tok), jnp.float32)
        final_got[FAR - 1] = jnp.zeros((heads, 2, row_tok), jnp.float32)
        term_got[FAR - 1] = jnp.zeros((heads, HEAD_DIM, row_tok), LOW)

    own_clip = clip_ref[position]
    core_valid = clip_ref[core_row] == own_clip
    far_valid = has_far & (clip_ref[far_row] == own_clip)
    valid = (True, core_valid, far_valid)

    step_q = QUERY_CHUNK if row_tok % QUERY_CHUNK == 0 else row_tok
    columns = [pl.ds(start, step_q) for start in range(0, row_tok, step_q)]
    rows = [pl.ds(start, KEY_CHUNK) for start in range(0, row_tok, KEY_CHUNK)]

    def slot_of(head, role):
        if role == OWN:
            return lax.rem(head, OWN_SLOTS)
        return OWN_SLOTS + 2 * (role - 1) + lax.rem(head, 2)

    def fold(value, op):
        return op(value.reshape(KEY_CHUNK // LANES, LANES, step_q), axis=0)

    def first_products(head, role, column):
        slot = slot_of(head, role)
        scores[:, column] = product(k_all[head], q_all[role, head, column, :], 1, 1)
        dprobs[slot, :, column] = product(v_all[head], g_all[role, head, column, :], 1, 1)

    def first_pass(head, role, column):
        slot = slot_of(head, role)
        top = None
        for row in rows:
            piece = fold(scores[row, column], jnp.max)
            top = piece if top is None else jnp.maximum(top, piece)
        top = jnp.max(top, axis=0, keepdims=True) * SCALE_LOG2
        mass = jnp.zeros((LANES, step_q), jnp.float32)
        delta = jnp.zeros((LANES, step_q), jnp.float32)
        for row in rows:
            weight = jnp.exp2(scores[row, column] * SCALE_LOG2 - top)
            weights[slot, row, column] = weight.astype(LOW)
            mass = mass + fold(weight, jnp.sum)
            delta = delta + fold(weight * dprobs[slot, row, column], jnp.sum)
        mass = jnp.sum(mass, axis=0, keepdims=True)
        delta = jnp.sum(delta, axis=0, keepdims=True)
        tops[role, head, :, column] = top
        part[role, head, 0:1, column] = top + jnp.log2(mass)
        part[role, head, 1:2, column] = delta / mass

    def second_pass(head, role, column):
        slot = slot_of(head, role)
        stats = final if role == OWN else final_got.at[role - 1]
        scale = jnp.exp2(tops[role, head, :, column] - stats[head, 0:1, column])
        if role != OWN:
            scale = jnp.where(valid[role], scale, 0.0)
        scale = scale.astype(LOW)
        delta = stats[head, 1:2, column]
        for row in rows:
            prob = weights[slot, row, column] * scale
            probs[row, column] = prob
            dscores[row, column] = prob * (dprobs[slot, row, column] - delta).astype(LOW)

    def query_product(head, role, column):
        piece = product(k_all[head], dscores[:, column], 0, 0)
        if role == OWN:
            dq_own[head, :, column] = piece
        else:
            term[role - 1, head, :, column] = piece.astype(LOW)

    def key_products(head, role, first, last):
        value_term = product(probs[...], g_all[role, head], 1, 0)
        key_term = product(dscores[...], q_all[role, head], 1, 0)
        if not first:
            value_term = value_term + total[1]
            key_term = key_term + total[0]
        if last:
            result[1, head] = (key_term * SCALE).astype(LOW)
            result[2, head] = value_term.astype(LOW)
        else:
            total[0] = key_term
            total[1] = value_term

    def step(early, late, first=False, last=False):
        for column in columns:
            if early is not None:
                first_products(*early, column)
            if late is not None:
                second_pass(*late, column)
            if early is not None:
                first_pass(*early, column)
            if late is not None:
                query_product(*late, column)
        if late is not None:
            key_products(*late, first, last)

    def wait_queries(head, role):
        def wait():
            q_copy(head, role).wait_recv()
            g_copy(head, role).wait_recv()
        if role == FAR:
            pl.when(has_far)(wait)
        else:
            wait()

    def on(role, action):
        if role == FAR:
            pl.when(has_far)(action)
        else:
            action()

    def merge(head):
        each_partner(lambda role: part_copy(head, role).wait_recv())
        logs = [part[OWN, head, 0:1, :]]
        deltas = [part[OWN, head, 1:2, :]]
        for role in (CORE, FAR):
            logs.append(jnp.where(valid[role], part_got[role - 1, head, 0:1, :], -jnp.inf))
            deltas.append(part_got[role - 1, head, 1:2, :])
        top = jnp.maximum(jnp.maximum(logs[0], logs[1]), logs[2])
        shares = [jnp.exp2(log - top) for log in logs]
        mass = shares[0] + shares[1] + shares[2]
        delta = shares[0] * deltas[0] + shares[1] * deltas[1] + shares[2] * deltas[2]
        final[head, 0:1, :] = top + jnp.log2(mass)
        final[head, 1:2, :] = delta / mass
        far_first(lambda role: final_copy(head, role).start())

    def finish_queries(head):
        each_partner(lambda role: term_copy(head, role).wait_recv())
        value = dq_own[head]
        for role in (CORE, FAR):
            value = value + term_got[role - 1, head].astype(jnp.float32)
        result[0, head] = (value * SCALE).T.astype(LOW)
        out_copy(head, 0).start()

    def finish_keys(head):
        out_copy(head, 1).start()
        out_copy(head, 2).start()

    for head in range(heads):
        load(head, 2).wait()
        load(head, 3).wait()

    def own_first(head, carry):
        step((head, OWN), None)
        return carry

    lax.fori_loop(0, min(OWN_SLOTS, heads), own_first, 0)
    wait_queries(0, FAR)
    step((0, FAR), None)
    on(FAR, lambda: part_copy(0, FAR).start())
    if heads > 2:
        send_q(2)
    wait_queries(0, CORE)
    step((0, CORE), None)
    part_copy(0, CORE).start()
    merge(0)
    if heads > 2:
        send_g(2)

    def one_head(head, carry):
        wait_queries(head + 1, FAR)
        step((head + 1, FAR), (head, OWN), first=True)
        on(FAR, lambda: part_copy(head + 1, FAR).start())

        @pl.when(head + 3 < heads)
        def _():
            send_q(head + 3)

        @pl.when(head + OWN_SLOTS < heads)
        def _():
            step((head + OWN_SLOTS, OWN), None)

        wait_queries(head + 1, CORE)
        final_copy(head, CORE).wait_recv()
        step((head + 1, CORE), (head, CORE))
        part_copy(head + 1, CORE).start()
        term_copy(head, CORE).start()

        @pl.when(head + 3 < heads)
        def _():
            send_g(head + 3)

        on(FAR, lambda: final_copy(head, FAR).wait_recv())
        step(None, (head, FAR), last=True)
        finish_keys(head)
        merge(head + 1)
        on(FAR, lambda: term_copy(head, FAR).start())

        @pl.when(head >= 2)
        def _():
            finish_queries(head - 2)

        return carry

    lax.fori_loop(0, heads - 1, one_head, 0)
    end = heads - 1
    step(None, (end, OWN), first=True)
    on(FAR, lambda: final_copy(end, FAR).wait_recv())
    step(None, (end, FAR))
    on(FAR, lambda: term_copy(end, FAR).start())
    final_copy(end, CORE).wait_recv()
    step(None, (end, CORE), last=True)
    term_copy(end, CORE).start()
    finish_keys(end)
    for head in range(max(heads - 3, 0), heads):
        finish_queries(head)

    def drain(head, carry):
        def wait(role):
            q_copy(head, role).wait_send()
            g_copy(head, role).wait_send()
            part_copy(head, role).wait_send()
            final_copy(head, role).wait_send()
            term_copy(head, role).wait_send()
        each_partner(wait)
        for which in range(3):
            out_copy(head, which).wait()
        return carry

    lax.fori_loop(0, heads, drain, 0)


def per_device(queries, keys_in, values, grad_out, clip_ids):
    row_tok, width = queries.shape
    heads = width // HEAD_DIM
    shape = jax.ShapeDtypeStruct((row_tok, width), LOW)
    anywhere = pl.BlockSpec(memory_space=pl.ANY)
    wide = jnp.float32
    slots = OWN_SLOTS + 4
    dma = pltpu.SemaphoreType.DMA
    return pl.pallas_call(
        attention_kernel,
        out_shape=(shape, shape, shape),
        in_specs=[pl.BlockSpec(memory_space=pltpu.SMEM)] + [anywhere] * 4,
        out_specs=(anywhere, anywhere, anywhere),
        scratch_shapes=[
            pltpu.VMEM((3, heads, row_tok, HEAD_DIM), LOW),
            pltpu.VMEM((3, heads, row_tok, HEAD_DIM), LOW),
            pltpu.VMEM((heads, row_tok, HEAD_DIM), LOW),
            pltpu.VMEM((heads, row_tok, HEAD_DIM), LOW),
            pltpu.VMEM((row_tok, row_tok), wide),
            pltpu.VMEM((slots, row_tok, row_tok), wide),
            pltpu.VMEM((slots, row_tok, row_tok), LOW),
            pltpu.VMEM((row_tok, row_tok), LOW),
            pltpu.VMEM((row_tok, row_tok), LOW),
            pltpu.VMEM((3, heads, 1, row_tok), wide),
            pltpu.VMEM((3, heads, 2, row_tok), wide),
            pltpu.VMEM((2, heads, 2, row_tok), wide),
            pltpu.VMEM((heads, 2, row_tok), wide),
            pltpu.VMEM((2, heads, 2, row_tok), wide),
            pltpu.VMEM((2, heads, HEAD_DIM, row_tok), LOW),
            pltpu.VMEM((2, heads, HEAD_DIM, row_tok), LOW),
            pltpu.VMEM((heads, HEAD_DIM, row_tok), wide),
            pltpu.VMEM((2, row_tok, HEAD_DIM), wide),
            pltpu.VMEM((3, heads, row_tok, HEAD_DIM), LOW),
            dma((4, heads)),
            dma((2, 2, heads)), dma((2, 2, heads)),
            dma((2, heads)), dma((2, heads)),
            dma((2, heads)), dma((2, heads)),
            dma((2, heads)), dma((2, heads)),
            dma((3, heads)),
        ],
        compiler_params=pltpu.CompilerParams(
            collective_id=0, has_side_effects=True, vmem_limit_bytes=58 * 1024 * 1024
        ),
    )(clip_ids, queries, keys_in, values, grad_out)


def solution(mesh):
    tokens = P(("groups", "ctx", "rep"), "head")
    return jax.shard_map(
        per_device,
        mesh=mesh,
        in_specs=(tokens, tokens, tokens, tokens, P("groups")),
        out_specs=(tokens, tokens, tokens),
        check_vma=False,
    )
```

```python
import math

import jax
import jax.numpy as jnp
from jax import lax
from jax.experimental import pallas as pl
from jax.experimental.pallas import tpu as pltpu
from jax.sharding import PartitionSpec as P

HEAD_DIM = 128
KEY_CHUNK = 64
QUERY_CHUNK = 256
LANES = 8
SLOTS = (3, 4, 1)
PIECES = 2
SCALE = HEAD_DIM ** -0.5
SCALE_LOG2 = SCALE * math.log2(math.e)
MESH = pl.DeviceIdType.MESH
OWN, CORE, FAR = 0, 1, 2
LOW = jnp.bfloat16


def product(left, right, left_axis, right_axis):
    return lax.dot_general(
        left, right, (((left_axis,), (right_axis,)), ((), ())),
        preferred_element_type=jnp.float32,
    )


def attention_kernel(
    clip_ref, q_hbm, k_hbm, v_hbm, g_hbm, dq_hbm, dk_hbm, dv_hbm,
    q_all, g_all, k_all, v_all, scores, own_dprobs, core_dprobs, far_dprobs,
    own_weights, core_weights, far_weights, probs, dscores,
    tops, part, part_got, lead, lead_got, final, final_got, far_final, term, term_got, dq_own, total, result,
    load_sem, qg_send, qg_recv, part_send, part_recv, lead_send, lead_recv, final_send, final_recv,
    term_send, term_recv, out_sem,
):
    heads, row_tok, _ = k_all.shape
    reps = lax.axis_size("rep")
    count = lax.axis_size("ctx") * reps
    rep = lax.axis_index("rep")
    position = lax.axis_index("ctx") * reps + rep
    core_row = position + 1 - 2 * rep
    far_row = position - 1 + 2 * rep
    has_far = (far_row >= 0) & (far_row < count)
    far_row = jnp.clip(far_row, 0, count - 1)

    def device(index):
        return {"ctx": index // reps, "rep": lax.rem(index, reps)}

    partners = (device(core_row), device(far_row))

    def each_partner(action):
        action(CORE)

        @pl.when(has_far)
        def _():
            action(FAR)

    def remote(source, target, send, recv, role):
        return pltpu.make_async_remote_copy(
            src_ref=source, dst_ref=target, send_sem=send, recv_sem=recv,
            device_id=partners[role - 1], device_id_type=MESH,
        )

    def q_copy(head, role):
        return remote(q_all.at[OWN, head], q_all.at[role, head],
                      qg_send.at[0, role - 1, head], qg_recv.at[0, role - 1, head], role)

    def g_copy(head, role):
        return remote(g_all.at[OWN, head], g_all.at[role, head],
                      qg_send.at[1, role - 1, head], qg_recv.at[1, role - 1, head], role)

    def part_copy(head, role):
        return remote(part.at[role, head], part_got.at[role - 1, head],
                      part_send.at[role - 1, head], part_recv.at[role - 1, head], role)

    def lead_copy(head):
        return remote(lead.at[head], lead_got.at[head], lead_send.at[head], lead_recv.at[head], FAR)

    def final_copy(head):
        return remote(final.at[head], final_got.at[head], final_send.at[head], final_recv.at[head], CORE)

    def term_copy(head, role):
        return remote(term.at[role - 1, head], term_got.at[role - 1, head],
                      term_send.at[role - 1, head], term_recv.at[role - 1, head], role)

    def strip(head):
        return pl.ds(pl.multiple_of(head * HEAD_DIM, HEAD_DIM), HEAD_DIM)

    def out_copy(head, which):
        target = (dq_hbm, dk_hbm, dv_hbm)[which]
        return pltpu.make_async_copy(
            result.at[which, head], target.at[:, strip(head)], out_sem.at[which, head]
        )

    def load(head, which):
        source = (q_hbm, g_hbm, k_hbm, v_hbm)[which]
        target = (q_all.at[OWN, head], g_all.at[OWN, head], k_all.at[head], v_all.at[head])[which]
        return pltpu.make_async_copy(
            source.at[:, strip(head)], target, load_sem.at[which, head]
        )

    def send_queries(head, role):
        q_copy(head, role).start()
        g_copy(head, role).start()

    def on_far(action):
        pl.when(has_far)(action)

    barrier = pltpu.get_barrier_semaphore()
    each_partner(lambda role: pl.semaphore_signal(
        barrier, inc=1, device_id=partners[role - 1], device_id_type=MESH))
    for head in range(heads):
        for which in range(4):
            load(head, which).start()
    pl.semaphore_wait(barrier, 1 + has_far.astype(jnp.int32))
    for head in range(heads):
        load(head, 0).wait()
        load(head, 1).wait()
        if head == 0:
            on_far(lambda: send_queries(0, FAR))
        if head < 3:
            send_queries(head, CORE)

    @pl.when(jnp.logical_not(has_far))
    def _():
        q_all[FAR] = jnp.zeros((heads, row_tok, HEAD_DIM), LOW)
        g_all[FAR] = jnp.zeros((heads, row_tok, HEAD_DIM), LOW)
        part_got[FAR - 1] = jnp.zeros((heads, 2, row_tok), jnp.float32)
        lead_got[...] = jnp.zeros((heads, 2, row_tok), jnp.float32)
        term_got[FAR - 1] = jnp.zeros((heads, HEAD_DIM, row_tok), LOW)

    own_clip = clip_ref[position]
    core_valid = clip_ref[core_row] == own_clip
    far_valid = has_far & (clip_ref[far_row] == own_clip)
    valid = (True, core_valid, far_valid)

    step_q = QUERY_CHUNK if row_tok % QUERY_CHUNK == 0 else row_tok
    columns = [pl.ds(start, step_q) for start in range(0, row_tok, step_q)]
    rows = [pl.ds(start, KEY_CHUNK) for start in range(0, row_tok, KEY_CHUNK)]

    all_dprobs = (own_dprobs, core_dprobs, far_dprobs)
    all_weights = (own_weights, core_weights, far_weights)

    def held(head, role):
        slot = lax.rem(head, all_weights[role].shape[0])
        return all_weights[role].at[slot], all_dprobs[role].at[slot]

    def fold(value, op):
        return op(value.reshape(KEY_CHUNK // LANES, LANES, step_q), axis=0)

    def first_products(head, role, column):
        _, dprobs = held(head, role)
        scores[:, column] = product(k_all[head], q_all[role, head, column, :], 1, 1)
        dprobs[:, column] = product(v_all[head], g_all[role, head, column, :], 1, 1)

    def first_pass(head, role, column):
        weights, dprobs = held(head, role)
        top = None
        for row in rows:
            piece = fold(scores[row, column], jnp.max)
            top = piece if top is None else jnp.maximum(top, piece)
        top = jnp.max(top, axis=0, keepdims=True) * SCALE_LOG2
        mass = jnp.zeros((LANES, step_q), jnp.float32)
        delta = jnp.zeros((LANES, step_q), jnp.float32)
        for row in rows:
            weight = jnp.exp2(scores[row, column] * SCALE_LOG2 - top)
            weights[row, column] = weight.astype(LOW)
            mass = mass + fold(weight, jnp.sum)
            delta = delta + fold(weight * dprobs[row, column], jnp.sum)
        mass = jnp.sum(mass, axis=0, keepdims=True)
        delta = jnp.sum(delta, axis=0, keepdims=True)
        tops[role, head, :, column] = top
        part[role, head, 0:1, column] = top + jnp.log2(mass)
        part[role, head, 1:2, column] = delta / mass

    def second_pass(head, role, column):
        weights, dprobs = held(head, role)
        stats = (final, final_got, far_final)[role]
        scale = jnp.exp2(tops[role, head, :, column] - stats[head, 0:1, column])
        if role != OWN:
            scale = jnp.where(valid[role], scale, 0.0)
        scale = scale.astype(LOW)
        delta = stats[head, 1:2, column]
        for row in rows:
            prob = weights[row, column] * scale
            probs[row, column] = prob
            dscores[row, column] = prob * (dprobs[row, column] - delta).astype(LOW)

    def query_product(head, role, column):
        piece = product(k_all[head], dscores[:, column], 0, 0)
        if role == OWN:
            dq_own[head, :, column] = piece
        else:
            term[role - 1, head, :, column] = piece.astype(LOW)

    def key_products(head, role):
        value_term = product(probs[...], g_all[role, head], 1, 0)
        key_term = product(dscores[...], q_all[role, head], 1, 0)
        slot = lax.rem(head, 2)
        if role != FAR:
            value_term = value_term + total[slot, 1]
            key_term = key_term + total[slot, 0]
        if role == CORE:
            result[1, head] = (key_term * SCALE).astype(LOW)
            result[2, head] = value_term.astype(LOW)
        else:
            total[slot, 0] = key_term
            total[slot, 1] = value_term

    def step(early, late):
        for column in columns:
            if early is not None:
                first_products(*early, column)
            if late is not None:
                second_pass(*late, column)
            if early is not None:
                first_pass(*early, column)
            if late is not None:
                query_product(*late, column)
        if late is not None:
            key_products(*late)

    def wait_queries(head, role):
        def wait():
            q_copy(head, role).wait_recv()
            g_copy(head, role).wait_recv()
        if role == FAR:
            on_far(wait)
        else:
            wait()

    def merged(first, second, second_valid):
        log, other = first[0:1, :], jnp.where(second_valid, second[0:1, :], -jnp.inf)
        top = jnp.maximum(log, other)
        share, other_share = jnp.exp2(log - top), jnp.exp2(other - top)
        mass = share + other_share
        delta = share * first[1:2, :] + other_share * second[1:2, :]
        return top + jnp.log2(mass), delta / mass

    def send_lead(head):
        part_copy(head, CORE).wait_recv()
        lead[head, 0:1, :], lead[head, 1:2, :] = merged(
            part.at[OWN, head], part_got.at[CORE - 1, head], core_valid)
        on_far(lambda: lead_copy(head).start())

    def settle_far(head):
        on_far(lambda: lead_copy(head).wait_recv())
        far_final[head, 0:1, :], far_final[head, 1:2, :] = merged(
            lead_got.at[head], part.at[FAR, head], True)

    def settle_own(head):
        on_far(lambda: part_copy(head, FAR).wait_recv())
        final[head, 0:1, :], final[head, 1:2, :] = merged(
            lead.at[head], part_got.at[FAR - 1, head], far_valid)
        final_copy(head).start()

    def finish_queries(head):
        each_partner(lambda role: term_copy(head, role).wait_recv())
        value = dq_own[head]
        for role in (CORE, FAR):
            value = value + term_got[role - 1, head].astype(jnp.float32)
        result[0, head] = (value * SCALE).T.astype(LOW)
        out_copy(head, 0).start()

    def finish_keys(head):
        out_copy(head, 1).start()
        out_copy(head, 2).start()

    for head in range(heads):
        load(head, 2).wait()
        load(head, 3).wait()

    def begin(head):
        wait_queries(head, CORE)
        step((head, CORE), None)
        part_copy(head, CORE).start()
        step((head, OWN), None)
        send_lead(head)

    def one_head(head, has_late, has_early):
        if has_late:
            settle_own(head - 1)
        wait_queries(head, FAR)
        step((head, FAR), (head - 1, OWN) if has_late else None)

        @pl.when(has_far)
        def _():
            part_copy(head, FAR).start()
            if has_late:
                term_copy(head - 1, FAR).start()
            if has_early:
                send_queries(head + 2, FAR)

        settle_far(head)
        if has_early:
            wait_queries(head + 2, CORE)
        step((head + 2, CORE) if has_early else None, (head, FAR))
        if has_early:
            part_copy(head + 2, CORE).start()

            @pl.when(head + 3 < heads)
            def _():
                send_queries(head + 3, CORE)
        if has_late:
            final_copy(head - 1).wait_recv()
        step((head + 2, OWN) if has_early else None, (head - 1, CORE) if has_late else None)
        if has_late:
            term_copy(head - 1, CORE).start()
            finish_keys(head - 1)
        if has_early:
            send_lead(head + 2)

    begin(0)
    on_far(lambda: send_queries(1, FAR))
    begin(1)
    one_head(0, False, True)

    def middle(head, carry):
        one_head(head, True, True)

        @pl.when(head >= 2)
        def _():
            finish_queries(head - 2)

        return carry

    lax.fori_loop(1, heads - 2, middle, 0)

    def ending(head, carry):
        one_head(head, True, False)
        finish_queries(head - 2)
        return carry

    lax.fori_loop(heads - 2, heads, ending, 0)
    end = heads - 1
    on_far(lambda: term_copy(end, FAR).start())
    settle_own(end)
    step(None, (end, OWN))
    finish_queries(end - 1)
    final_copy(end).wait_recv()
    step(None, (end, CORE))
    term_copy(end, CORE).start()
    finish_keys(end)
    finish_queries(end)

    def drain(head, carry):
        def wait(role):
            q_copy(head, role).wait_send()
            g_copy(head, role).wait_send()
            part_copy(head, role).wait_send()
            term_copy(head, role).wait_send()
            if role == FAR:
                lead_copy(head).wait_send()
        each_partner(wait)
        final_copy(head).wait_send()
        for which in range(3):
            out_copy(head, which).wait()
        return carry

    lax.fori_loop(0, heads, drain, 0)


def place_kernel(*refs):
    sources, targets, (held, in_sem, out_sem) = refs[:3], refs[3:6], refs[6:]
    size = held.shape[1] // PIECES
    pieces = []
    for which in range(3):
        for piece in range(PIECES):
            part = pl.ds(piece * size, size)
            pieces.append((
                pltpu.make_async_copy(
                    sources[which].at[part], held.at[which, part], in_sem.at[which, piece]
                ),
                pltpu.make_async_copy(
                    held.at[which, part], targets[which].at[part], out_sem.at[which, piece]
                ),
            ))
    for copy_in, _ in pieces:
        copy_in.start()
    for copy_in, copy_out in pieces:
        copy_in.wait()
        copy_out.start()
    for _, copy_out in pieces:
        copy_out.wait()


def per_device(queries, keys_in, values, grad_out, clip_ids):
    row_tok, width = queries.shape
    heads = width // HEAD_DIM
    shape = jax.ShapeDtypeStruct((row_tok, width), LOW)
    anywhere = pl.BlockSpec(memory_space=pl.ANY)
    wide = jnp.float32
    dma = pltpu.SemaphoreType.DMA
    grads = pl.pallas_call(
        attention_kernel,
        out_shape=(shape, shape, shape),
        in_specs=[pl.BlockSpec(memory_space=pltpu.SMEM)] + [anywhere] * 4,
        out_specs=(anywhere, anywhere, anywhere),
        scratch_shapes=[
            pltpu.VMEM((3, heads, row_tok, HEAD_DIM), LOW),
            pltpu.VMEM((3, heads, row_tok, HEAD_DIM), LOW),
            pltpu.VMEM((heads, row_tok, HEAD_DIM), LOW),
            pltpu.VMEM((heads, row_tok, HEAD_DIM), LOW),
            pltpu.VMEM((row_tok, row_tok), wide),
            *(pltpu.VMEM((slots, row_tok, row_tok), wide) for slots in SLOTS),
            *(pltpu.VMEM((slots, row_tok, row_tok), LOW) for slots in SLOTS),
            pltpu.VMEM((row_tok, row_tok), LOW),
            pltpu.VMEM((row_tok, row_tok), LOW),
            pltpu.VMEM((3, heads, 1, row_tok), wide),
            pltpu.VMEM((3, heads, 2, row_tok), wide),
            pltpu.VMEM((2, heads, 2, row_tok), wide),
            *[pltpu.VMEM((heads, 2, row_tok), wide)] * 5,
            pltpu.VMEM((2, heads, HEAD_DIM, row_tok), LOW),
            pltpu.VMEM((2, heads, HEAD_DIM, row_tok), LOW),
            pltpu.VMEM((heads, HEAD_DIM, row_tok), wide),
            pltpu.VMEM((2, 2, row_tok, HEAD_DIM), wide),
            pltpu.VMEM((3, heads, row_tok, HEAD_DIM), LOW),
            dma((4, heads)),
            dma((2, 2, heads)), dma((2, 2, heads)),
            dma((2, heads)), dma((2, heads)),
            dma((heads,)), dma((heads,)),
            dma((heads,)), dma((heads,)),
            dma((2, heads)), dma((2, heads)),
            dma((3, heads)),
        ],
        compiler_params=pltpu.CompilerParams(
            collective_id=0, has_side_effects=True, vmem_limit_bytes=58 * 1024 * 1024
        ),
    )(clip_ids, queries, keys_in, values, grad_out)
    return pl.pallas_call(
        place_kernel,
        out_shape=(shape, shape, shape),
        in_specs=[anywhere] * 3,
        out_specs=(anywhere, anywhere, anywhere),
        scratch_shapes=[
            pltpu.VMEM((3, row_tok, width), LOW), dma((3, PIECES)), dma((3, PIECES)),
        ],
        compiler_params=pltpu.CompilerParams(vmem_limit_bytes=58 * 1024 * 1024),
    )(*grads)


def solution(mesh):
    tokens = P(("groups", "ctx", "rep"), "head")
    return jax.shard_map(
        per_device,
        mesh=mesh,
        in_specs=(tokens, tokens, tokens, tokens, P("groups")),
        out_specs=(tokens, tokens, tokens),
        check_vma=False,
    )
```

```python
import math

import jax
import jax.numpy as jnp
from jax import lax
from jax.experimental import pallas as pl
from jax.experimental.pallas import tpu as pltpu
from jax.sharding import PartitionSpec as P

HEAD_DIM = 128
KEY_CHUNK = 64
QUERY_CHUNK = 256
LANES = 8
SLOTS = (3, 4, 1)
PIECES = 2
SCALE = HEAD_DIM ** -0.5
SCALE_LOG2 = SCALE * math.log2(math.e)
MESH = pl.DeviceIdType.MESH
OWN, CORE, FAR = 0, 1, 2
LOW = jnp.bfloat16


def product(left, right, left_axis, right_axis):
    return lax.dot_general(
        left, right, (((left_axis,), (right_axis,)), ((), ())),
        preferred_element_type=jnp.float32,
    )


def attention_kernel(
    clip_ref, q_hbm, k_hbm, v_hbm, g_hbm, dq_hbm, dk_hbm, dv_hbm,
    q_all, g_all, k_all, v_all, scores, own_dprobs, core_dprobs, far_dprobs,
    own_weights, core_weights, far_weights, probs, dscores,
    own_tops, core_tops, far_tops, part, part_got, lead, lead_got, final, final_got, far_final, term, term_got, dq_own, total, result,
    load_sem, qg_send, qg_recv, part_send, part_recv, lead_send, lead_recv, final_send, final_recv,
    term_send, term_recv, out_sem,
):
    heads, row_tok, _ = k_all.shape
    reps = lax.axis_size("rep")
    count = lax.axis_size("ctx") * reps
    rep = lax.axis_index("rep")
    position = lax.axis_index("ctx") * reps + rep
    core_row = position + 1 - 2 * rep
    far_row = position - 1 + 2 * rep
    has_far = (far_row >= 0) & (far_row < count)
    far_row = jnp.clip(far_row, 0, count - 1)

    def device(index):
        return {"ctx": index // reps, "rep": lax.rem(index, reps)}

    partners = (device(core_row), device(far_row))

    def each_partner(action):
        action(CORE)

        @pl.when(has_far)
        def _():
            action(FAR)

    def remote(source, target, send, recv, role):
        return pltpu.make_async_remote_copy(
            src_ref=source, dst_ref=target, send_sem=send, recv_sem=recv,
            device_id=partners[role - 1], device_id_type=MESH,
        )

    def q_copy(head, role):
        return remote(q_all.at[OWN, head], q_all.at[role, head],
                      qg_send.at[0, role - 1, head], qg_recv.at[0, role - 1, head], role)

    def g_copy(head, role):
        return remote(g_all.at[OWN, head], g_all.at[role, head],
                      qg_send.at[1, role - 1, head], qg_recv.at[1, role - 1, head], role)

    def part_copy(head, role):
        return remote(part.at[role, head], part_got.at[role - 1, head],
                      part_send.at[role - 1, head], part_recv.at[role - 1, head], role)

    def lead_copy(head):
        return remote(lead.at[head], lead_got.at[head], lead_send.at[head], lead_recv.at[head], FAR)

    def final_copy(head):
        return remote(final.at[head], final_got.at[head], final_send.at[head], final_recv.at[head], CORE)

    def term_copy(head, role):
        return remote(term.at[role - 1, head], term_got.at[role - 1, head],
                      term_send.at[role - 1, head], term_recv.at[role - 1, head], role)

    def strip(head):
        return pl.ds(pl.multiple_of(head * HEAD_DIM, HEAD_DIM), HEAD_DIM)

    def out_copy(head, which):
        target = (dq_hbm, dk_hbm, dv_hbm)[which]
        return pltpu.make_async_copy(
            result.at[which, head], target.at[:, strip(head)], out_sem.at[which, head]
        )

    def load(head, which):
        source = (q_hbm, g_hbm, k_hbm, v_hbm)[which]
        target = (q_all.at[OWN, head], g_all.at[OWN, head], k_all.at[head], v_all.at[head])[which]
        return pltpu.make_async_copy(
            source.at[:, strip(head)], target, load_sem.at[which, head]
        )

    def send_queries(head, role):
        q_copy(head, role).start()
        g_copy(head, role).start()

    def on_far(action):
        pl.when(has_far)(action)

    barrier = pltpu.get_barrier_semaphore()
    each_partner(lambda role: pl.semaphore_signal(
        barrier, inc=1, device_id=partners[role - 1], device_id_type=MESH))
    for head in range(heads):
        for which in range(4):
            load(head, which).start()
    pl.semaphore_wait(barrier, 1 + has_far.astype(jnp.int32))
    for head in range(heads):
        load(head, 0).wait()
        load(head, 1).wait()
        if head == 0:
            on_far(lambda: send_queries(0, FAR))
        if head < 3:
            send_queries(head, CORE)

    @pl.when(jnp.logical_not(has_far))
    def _():
        q_all[FAR] = jnp.zeros((heads, row_tok, HEAD_DIM), LOW)
        g_all[FAR] = jnp.zeros((heads, row_tok, HEAD_DIM), LOW)
        part_got[FAR - 1] = jnp.zeros((heads, 2, row_tok), jnp.float32)
        lead_got[...] = jnp.zeros((heads, 2, row_tok), jnp.float32)
        term_got[FAR - 1] = jnp.zeros((heads, HEAD_DIM, row_tok), LOW)

    own_clip = clip_ref[position]
    core_valid = clip_ref[core_row] == own_clip
    far_valid = has_far & (clip_ref[far_row] == own_clip)
    valid = (True, core_valid, far_valid)

    step_q = QUERY_CHUNK if row_tok % QUERY_CHUNK == 0 else row_tok
    columns = [pl.ds(start, step_q) for start in range(0, row_tok, step_q)]
    rows = [pl.ds(start, KEY_CHUNK) for start in range(0, row_tok, KEY_CHUNK)]

    all_dprobs = (own_dprobs, core_dprobs, far_dprobs)
    all_weights = (own_weights, core_weights, far_weights)
    tops = (own_tops, core_tops, far_tops)

    def held(head, role):
        slot = lax.rem(head, all_weights[role].shape[0])
        return all_weights[role].at[slot], all_dprobs[role].at[slot]

    def fold(value, op):
        return op(value.reshape(KEY_CHUNK // LANES, LANES, step_q), axis=0)

    def first_products(head, role, column):
        _, dprobs = held(head, role)
        scores[:, column] = product(k_all[head], q_all[role, head, column, :], 1, 1)
        dprobs[:, column] = product(v_all[head], g_all[role, head, column, :], 1, 1)

    def first_pass(head, role, column):
        weights, dprobs = held(head, role)
        top = None
        for row in rows:
            piece = fold(scores[row, column], jnp.max)
            top = piece if top is None else jnp.maximum(top, piece)
        top = jnp.max(top, axis=0, keepdims=True) * SCALE_LOG2
        mass = jnp.zeros((LANES, step_q), jnp.float32)
        delta = jnp.zeros((LANES, step_q), jnp.float32)
        for row in rows:
            weight = jnp.exp2(scores[row, column] * SCALE_LOG2 - top)
            weights[row, column] = weight.astype(LOW)
            mass = mass + fold(weight, jnp.sum)
            delta = delta + fold(weight * dprobs[row, column], jnp.sum)
        mass = jnp.sum(mass, axis=0, keepdims=True)
        delta = jnp.sum(delta, axis=0, keepdims=True)
        tops[role][head, :, column] = top
        part[role, head, 0:1, column] = top + jnp.log2(mass)
        part[role, head, 1:2, column] = delta / mass

    def second_pass(head, role, column):
        weights, dprobs = held(head, role)
        stats = (final, final_got, far_final)[role]
        scale = jnp.exp2(tops[role][head, :, column] - stats[head, 0:1, column])
        if role != OWN:
            scale = jnp.where(valid[role], scale, 0.0)
        scale = scale.astype(LOW)
        delta = stats[head, 1:2, column]
        for row in rows:
            prob = weights[row, column] * scale
            probs[row, column] = prob
            dscores[row, column] = prob * (dprobs[row, column] - delta).astype(LOW)

    def query_product(head, role, column):
        piece = product(k_all[head], dscores[:, column], 0, 0)
        if role == OWN:
            dq_own[head, :, column] = piece
        else:
            term[role - 1, head, :, column] = piece.astype(LOW)

    def key_products(head, role):
        value_term = product(probs[...], g_all[role, head], 1, 0)
        key_term = product(dscores[...], q_all[role, head], 1, 0)
        slot = lax.rem(head, 2)
        if role != FAR:
            value_term = value_term + total[slot, 1]
            key_term = key_term + total[slot, 0]
        if role == CORE:
            result[1, head] = (key_term * SCALE).astype(LOW)
            result[2, head] = value_term.astype(LOW)
        else:
            total[slot, 0] = key_term
            total[slot, 1] = value_term

    def step(early, late):
        for column in columns:
            if early is not None:
                first_products(*early, column)
            if late is not None:
                second_pass(*late, column)
            if early is not None:
                first_pass(*early, column)
            if late is not None:
                query_product(*late, column)
        if late is not None:
            key_products(*late)

    def wait_queries(head, role):
        def wait():
            q_copy(head, role).wait_recv()
            g_copy(head, role).wait_recv()
        if role == FAR:
            on_far(wait)
        else:
            wait()

    def merged(first, second, second_valid):
        log, other = first[0:1, :], jnp.where(second_valid, second[0:1, :], -jnp.inf)
        top = jnp.maximum(log, other)
        share, other_share = jnp.exp2(log - top), jnp.exp2(other - top)
        mass = share + other_share
        delta = share * first[1:2, :] + other_share * second[1:2, :]
        return top + jnp.log2(mass), delta / mass

    def send_lead(head):
        part_copy(head, CORE).wait_recv()
        lead[head, 0:1, :], lead[head, 1:2, :] = merged(
            part.at[OWN, head], part_got.at[CORE - 1, head], core_valid)
        on_far(lambda: lead_copy(head).start())

    def settle_far(head):
        on_far(lambda: lead_copy(head).wait_recv())
        far_final[head, 0:1, :], far_final[head, 1:2, :] = merged(
            lead_got.at[head], part.at[FAR, head], True)

    def settle_own(head):
        on_far(lambda: part_copy(head, FAR).wait_recv())
        final[head, 0:1, :], final[head, 1:2, :] = merged(
            lead.at[head], part_got.at[FAR - 1, head], far_valid)
        final_copy(head).start()

    def finish_queries(head):
        each_partner(lambda role: term_copy(head, role).wait_recv())
        value = dq_own[head]
        for role in (CORE, FAR):
            value = value + term_got[role - 1, head].astype(jnp.float32)
        result[0, head] = (value * SCALE).T.astype(LOW)
        out_copy(head, 0).start()

    def finish_keys(head):
        out_copy(head, 1).start()
        out_copy(head, 2).start()

    for head in range(heads):
        load(head, 2).wait()
        load(head, 3).wait()

    def begin(head):
        wait_queries(head, CORE)
        step((head, CORE), None)
        part_copy(head, CORE).start()
        step((head, OWN), None)
        send_lead(head)

    def one_head(head, has_late, has_early):
        if has_late:
            settle_own(head - 1)
        wait_queries(head, FAR)
        step((head, FAR), (head - 1, OWN) if has_late else None)

        @pl.when(has_far)
        def _():
            part_copy(head, FAR).start()
            if has_late:
                term_copy(head - 1, FAR).start()
            if has_early:
                send_queries(head + 2, FAR)

        settle_far(head)
        if has_early:
            wait_queries(head + 2, CORE)
        step((head + 2, CORE) if has_early else None, (head, FAR))
        if has_early:
            part_copy(head + 2, CORE).start()

            @pl.when(head + 3 < heads)
            def _():
                send_queries(head + 3, CORE)
        if has_late:
            final_copy(head - 1).wait_recv()
        step((head + 2, OWN) if has_early else None, (head - 1, CORE) if has_late else None)
        if has_late:
            term_copy(head - 1, CORE).start()
            finish_keys(head - 1)
        if has_early:
            send_lead(head + 2)

    begin(0)
    on_far(lambda: send_queries(1, FAR))
    begin(1)
    one_head(0, False, True)

    def middle(head, carry):
        one_head(head, True, True)

        @pl.when(head >= 2)
        def _():
            finish_queries(head - 2)

        return carry

    lax.fori_loop(1, heads - 2, middle, 0)

    def ending(head, carry):
        wait_queries(head, FAR)
        step((head, FAR), None)

        @pl.when(has_far)
        def _():
            part_copy(head, FAR).start()

            @pl.when(head == heads - 2)
            def _():
                term_copy(head - 1, FAR).start()

        settle_far(head)
        step(None, (head, FAR))
        on_far(lambda: term_copy(head, FAR).start())
        settle_own(head - 1)
        step(None, (head - 1, OWN))
        final_copy(head - 1).wait_recv()
        step(None, (head - 1, CORE))
        term_copy(head - 1, CORE).start()
        finish_keys(head - 1)
        finish_queries(head - 2)
        return carry

    lax.fori_loop(heads - 2, heads, ending, 0)
    end = heads - 1
    settle_own(end)
    step(None, (end, OWN))
    finish_queries(end - 1)
    final_copy(end).wait_recv()
    step(None, (end, CORE))
    term_copy(end, CORE).start()
    finish_keys(end)
    finish_queries(end)

    def drain(head, carry):
        def wait(role):
            q_copy(head, role).wait_send()
            g_copy(head, role).wait_send()
            part_copy(head, role).wait_send()
            term_copy(head, role).wait_send()
            if role == FAR:
                lead_copy(head).wait_send()
        each_partner(wait)
        final_copy(head).wait_send()
        for which in range(3):
            out_copy(head, which).wait()
        return carry

    lax.fori_loop(0, heads, drain, 0)


def place_kernel(*refs):
    sources, targets, (held, in_sem, out_sem) = refs[:3], refs[3:6], refs[6:]
    size = held.shape[1] // PIECES
    pieces = []
    for which in range(3):
        for piece in range(PIECES):
            part = pl.ds(piece * size, size)
            pieces.append((
                pltpu.make_async_copy(
                    sources[which].at[part], held.at[which, part], in_sem.at[which, piece]
                ),
                pltpu.make_async_copy(
                    held.at[which, part], targets[which].at[part], out_sem.at[which, piece]
                ),
            ))
    for copy_in, _ in pieces:
        copy_in.start()
    for copy_in, copy_out in pieces:
        copy_in.wait()
        copy_out.start()
    for _, copy_out in pieces:
        copy_out.wait()


def per_device(queries, keys_in, values, grad_out, clip_ids):
    row_tok, width = queries.shape
    heads = width // HEAD_DIM
    shape = jax.ShapeDtypeStruct((row_tok, width), LOW)
    anywhere = pl.BlockSpec(memory_space=pl.ANY)
    wide = jnp.float32
    dma = pltpu.SemaphoreType.DMA
    grads = pl.pallas_call(
        attention_kernel,
        out_shape=(shape, shape, shape),
        in_specs=[pl.BlockSpec(memory_space=pltpu.SMEM)] + [anywhere] * 4,
        out_specs=(anywhere, anywhere, anywhere),
        scratch_shapes=[
            pltpu.VMEM((3, heads, row_tok, HEAD_DIM), LOW),
            pltpu.VMEM((3, heads, row_tok, HEAD_DIM), LOW),
            pltpu.VMEM((heads, row_tok, HEAD_DIM), LOW),
            pltpu.VMEM((heads, row_tok, HEAD_DIM), LOW),
            pltpu.VMEM((row_tok, row_tok), wide),
            *(pltpu.VMEM((slots, row_tok, row_tok), wide) for slots in SLOTS),
            *(pltpu.VMEM((slots, row_tok, row_tok), LOW) for slots in SLOTS),
            pltpu.VMEM((row_tok, row_tok), LOW),
            pltpu.VMEM((row_tok, row_tok), LOW),
            *[pltpu.VMEM((heads, 1, row_tok), wide)] * 3,
            pltpu.VMEM((3, heads, 2, row_tok), wide),
            pltpu.VMEM((2, heads, 2, row_tok), wide),
            *[pltpu.VMEM((heads, 2, row_tok), wide)] * 5,
            pltpu.VMEM((2, heads, HEAD_DIM, row_tok), LOW),
            pltpu.VMEM((2, heads, HEAD_DIM, row_tok), LOW),
            pltpu.VMEM((heads, HEAD_DIM, row_tok), wide),
            pltpu.VMEM((2, 2, row_tok, HEAD_DIM), wide),
            pltpu.VMEM((3, heads, row_tok, HEAD_DIM), LOW),
            dma((4, heads)),
            dma((2, 2, heads)), dma((2, 2, heads)),
            dma((2, heads)), dma((2, heads)),
            dma((heads,)), dma((heads,)),
            dma((heads,)), dma((heads,)),
            dma((2, heads)), dma((2, heads)),
            dma((3, heads)),
        ],
        compiler_params=pltpu.CompilerParams(
            collective_id=0, has_side_effects=True, vmem_limit_bytes=58 * 1024 * 1024
        ),
    )(clip_ids, queries, keys_in, values, grad_out)
    return pl.pallas_call(
        place_kernel,
        out_shape=(shape, shape, shape),
        in_specs=[anywhere] * 3,
        out_specs=(anywhere, anywhere, anywhere),
        scratch_shapes=[
            pltpu.VMEM((3, row_tok, width), LOW), dma((3, PIECES)), dma((3, PIECES)),
        ],
        compiler_params=pltpu.CompilerParams(vmem_limit_bytes=58 * 1024 * 1024),
    )(*grads)


def solution(mesh):
    tokens = P(("groups", "ctx", "rep"), "head")
    return jax.shard_map(
        per_device,
        mesh=mesh,
        in_specs=(tokens, tokens, tokens, tokens, P("groups")),
        out_specs=(tokens, tokens, tokens),
        check_vma=False,
    )
```

```python
import math

import jax
import jax.numpy as jnp
from jax import lax
from jax.experimental import pallas as pl
from jax.experimental.pallas import tpu as pltpu
from jax.sharding import PartitionSpec as P

HEAD_DIM = 128
KEY_CHUNK = 64
QUERY_CHUNK = 256
LANES = 8
SLOTS = (3, 4, 1)
PIECES = 2
SCALE = HEAD_DIM ** -0.5
SCALE_LOG2 = SCALE * math.log2(math.e)
MESH = pl.DeviceIdType.MESH
OWN, CORE, FAR = 0, 1, 2
LOW = jnp.bfloat16


def product(left, right, left_axis, right_axis):
    return lax.dot_general(
        left, right, (((left_axis,), (right_axis,)), ((), ())),
        preferred_element_type=jnp.float32,
    )


def attention_kernel(
    clip_ref, q_hbm, k_hbm, v_hbm, g_hbm, dq_hbm, dk_hbm, dv_hbm,
    q_all, g_all, k_all, v_all, scores, own_dprobs, core_dprobs, far_dprobs,
    own_weights, core_weights, far_weights, probs, dscores,
    own_tops, core_tops, far_tops, part, part_got, lead, lead_got, final, final_got, far_final, term, term_got, dq_own, total, result,
    load_sem, qg_send, qg_recv, part_send, part_recv, lead_send, lead_recv, final_send, final_recv,
    term_send, term_recv, out_sem,
):
    heads, row_tok, _ = k_all.shape
    reps = lax.axis_size("rep")
    count = lax.axis_size("ctx") * reps
    rep = lax.axis_index("rep")
    position = lax.axis_index("ctx") * reps + rep
    core_row = position + 1 - 2 * rep
    far_row = position - 1 + 2 * rep
    has_far = (far_row >= 0) & (far_row < count)
    far_row = jnp.clip(far_row, 0, count - 1)

    def device(index):
        return {"ctx": index // reps, "rep": lax.rem(index, reps)}

    partners = (device(core_row), device(far_row))

    def each_partner(action):
        action(CORE)

        @pl.when(has_far)
        def _():
            action(FAR)

    def remote(source, target, send, recv, role):
        return pltpu.make_async_remote_copy(
            src_ref=source, dst_ref=target, send_sem=send, recv_sem=recv,
            device_id=partners[role - 1], device_id_type=MESH,
        )

    def q_copy(head, role):
        return remote(q_all.at[OWN, head], q_all.at[role, head],
                      qg_send.at[0, role - 1, head], qg_recv.at[0, role - 1, head], role)

    def g_copy(head, role):
        return remote(g_all.at[OWN, head], g_all.at[role, head],
                      qg_send.at[1, role - 1, head], qg_recv.at[1, role - 1, head], role)

    def part_copy(head, role):
        return remote(part.at[role, head], part_got.at[role - 1, head],
                      part_send.at[role - 1, head], part_recv.at[role - 1, head], role)

    def lead_copy(head):
        return remote(lead.at[head], lead_got.at[head], lead_send.at[head], lead_recv.at[head], FAR)

    def final_copy(head):
        return remote(final.at[head], final_got.at[head], final_send.at[head], final_recv.at[head], CORE)

    def term_copy(head, role):
        return remote(term.at[role - 1, head], term_got.at[role - 1, head],
                      term_send.at[role - 1, head], term_recv.at[role - 1, head], role)

    def strip(head):
        return pl.ds(pl.multiple_of(head * HEAD_DIM, HEAD_DIM), HEAD_DIM)

    def out_copy(head, which):
        target = (dq_hbm, dk_hbm, dv_hbm)[which]
        return pltpu.make_async_copy(
            result.at[which, head], target.at[:, strip(head)], out_sem.at[which, head]
        )

    def load(head, which):
        source = (q_hbm, g_hbm, k_hbm, v_hbm)[which]
        target = (q_all.at[OWN, head], g_all.at[OWN, head], k_all.at[head], v_all.at[head])[which]
        return pltpu.make_async_copy(
            source.at[:, strip(head)], target, load_sem.at[which, head]
        )

    def send_queries(head, role):
        q_copy(head, role).start()
        g_copy(head, role).start()

    def on_far(action):
        pl.when(has_far)(action)

    barrier = pltpu.get_barrier_semaphore()
    each_partner(lambda role: pl.semaphore_signal(
        barrier, inc=1, device_id=partners[role - 1], device_id_type=MESH))
    for head in range(heads):
        for which in range(4):
            load(head, which).start()
    pl.semaphore_wait(barrier, 1 + has_far.astype(jnp.int32))
    for head in range(heads):
        load(head, 0).wait()
        load(head, 1).wait()
        if head == 0:
            on_far(lambda: send_queries(0, FAR))
        if head < 3:
            send_queries(head, CORE)

    @pl.when(jnp.logical_not(has_far))
    def _():
        q_all[FAR] = jnp.zeros((heads, row_tok, HEAD_DIM), LOW)
        g_all[FAR] = jnp.zeros((heads, row_tok, HEAD_DIM), LOW)
        part_got[FAR - 1] = jnp.zeros((heads, 2, row_tok), jnp.float32)
        lead_got[...] = jnp.zeros((heads, 2, row_tok), jnp.float32)
        term_got[FAR - 1] = jnp.zeros((heads, HEAD_DIM, row_tok), LOW)

    own_clip = clip_ref[position]
    core_valid = clip_ref[core_row] == own_clip
    far_valid = has_far & (clip_ref[far_row] == own_clip)
    valid = (True, core_valid, far_valid)

    step_q = QUERY_CHUNK if row_tok % QUERY_CHUNK == 0 else row_tok
    columns = [pl.ds(start, step_q) for start in range(0, row_tok, step_q)]
    rows = [pl.ds(start, KEY_CHUNK) for start in range(0, row_tok, KEY_CHUNK)]

    all_dprobs = (own_dprobs, core_dprobs, far_dprobs)
    all_weights = (own_weights, core_weights, far_weights)
    tops = (own_tops, core_tops, far_tops)

    def held(head, role):
        slot = lax.rem(head, all_weights[role].shape[0])
        return all_weights[role].at[slot], all_dprobs[role].at[slot]

    def fold(value, op):
        return op(value.reshape(KEY_CHUNK // LANES, LANES, value.shape[1]), axis=0)

    def first_products(head, role, column):
        _, dprobs = held(head, role)
        scores[:, column] = product(k_all[head], q_all[role, head, column, :], 1, 1)
        dprobs[:, column] = product(v_all[head], g_all[role, head, column, :], 1, 1)

    def first_pass(head, role, column):
        weights, dprobs = held(head, role)
        top = None
        for row in rows:
            piece = fold(scores[row, column], jnp.max)
            top = piece if top is None else jnp.maximum(top, piece)
        top = jnp.max(top, axis=0, keepdims=True) * SCALE_LOG2
        mass = jnp.zeros((LANES, column.size), jnp.float32)
        delta = jnp.zeros((LANES, column.size), jnp.float32)
        for row in rows:
            weight = jnp.exp2(scores[row, column] * SCALE_LOG2 - top)
            weights[row, column] = weight.astype(LOW)
            mass = mass + fold(weight, jnp.sum)
            delta = delta + fold(weight * dprobs[row, column], jnp.sum)
        mass = jnp.sum(mass, axis=0, keepdims=True)
        delta = jnp.sum(delta, axis=0, keepdims=True)
        tops[role][head, :, column] = top
        part[role, head, 0:1, column] = top + jnp.log2(mass)
        part[role, head, 1:2, column] = delta / mass

    def second_pass(head, role, column):
        weights, dprobs = held(head, role)
        stats = (final, final_got, far_final)[role]
        scale = jnp.exp2(tops[role][head, :, column] - stats[head, 0:1, column])
        if role != OWN:
            scale = jnp.where(valid[role], scale, 0.0)
        scale = scale.astype(LOW)
        delta = stats[head, 1:2, column]
        for row in rows:
            prob = weights[row, column] * scale
            probs[row, column] = prob
            dscores[row, column] = prob * (dprobs[row, column] - delta).astype(LOW)

    def query_product(head, role, column):
        piece = product(k_all[head], dscores[:, column], 0, 0)
        if role == OWN:
            dq_own[head, :, column] = piece
        else:
            term[role - 1, head, :, column] = piece.astype(LOW)

    def key_products(head, role):
        value_term = product(probs[...], g_all[role, head], 1, 0)
        key_term = product(dscores[...], q_all[role, head], 1, 0)
        slot = lax.rem(head, 2)
        if role != FAR:
            value_term = value_term + total[slot, 1]
            key_term = key_term + total[slot, 0]
        if role == CORE:
            result[1, head] = (key_term * SCALE).astype(LOW)
            result[2, head] = value_term.astype(LOW)
        else:
            total[slot, 0] = key_term
            total[slot, 1] = value_term

    def step(early, late):
        for column in [pl.ds(0, row_tok)] if late is None else columns:
            if early is not None:
                first_products(*early, column)
            if late is not None:
                second_pass(*late, column)
            if early is not None:
                first_pass(*early, column)
            if late is not None:
                query_product(*late, column)
        if late is not None:
            key_products(*late)

    def wait_queries(head, role):
        def wait():
            q_copy(head, role).wait_recv()
            g_copy(head, role).wait_recv()
        if role == FAR:
            on_far(wait)
        else:
            wait()

    def merged(first, second, second_valid):
        log, other = first[0:1, :], jnp.where(second_valid, second[0:1, :], -jnp.inf)
        top = jnp.maximum(log, other)
        share, other_share = jnp.exp2(log - top), jnp.exp2(other - top)
        mass = share + other_share
        delta = share * first[1:2, :] + other_share * second[1:2, :]
        return top + jnp.log2(mass), delta / mass

    def send_lead(head):
        part_copy(head, CORE).wait_recv()
        lead[head, 0:1, :], lead[head, 1:2, :] = merged(
            part.at[OWN, head], part_got.at[CORE - 1, head], core_valid)
        on_far(lambda: lead_copy(head).start())

    def settle_far(head):
        on_far(lambda: lead_copy(head).wait_recv())
        far_final[head, 0:1, :], far_final[head, 1:2, :] = merged(
            lead_got.at[head], part.at[FAR, head], True)

    def settle_own(head):
        on_far(lambda: part_copy(head, FAR).wait_recv())
        final[head, 0:1, :], final[head, 1:2, :] = merged(
            lead.at[head], part_got.at[FAR - 1, head], far_valid)
        final_copy(head).start()

    def finish_queries(head):
        each_partner(lambda role: term_copy(head, role).wait_recv())
        value = dq_own[head]
        for role in (CORE, FAR):
            value = value + term_got[role - 1, head].astype(jnp.float32)
        result[0, head] = (value * SCALE).T.astype(LOW)
        out_copy(head, 0).start()

    def finish_keys(head):
        out_copy(head, 1).start()
        out_copy(head, 2).start()

    for head in range(heads):
        load(head, 2).wait()
        load(head, 3).wait()

    def begin(head):
        wait_queries(head, CORE)
        step((head, CORE), None)
        part_copy(head, CORE).start()
        step((head, OWN), None)
        send_lead(head)

    def one_head(head, has_late, has_early):
        if has_late:
            settle_own(head - 1)
        wait_queries(head, FAR)
        step((head, FAR), (head - 1, OWN) if has_late else None)

        @pl.when(has_far)
        def _():
            part_copy(head, FAR).start()
            if has_late:
                term_copy(head - 1, FAR).start()
            if has_early:
                send_queries(head + 2, FAR)

        settle_far(head)
        if has_early:
            wait_queries(head + 2, CORE)
        step((head + 2, CORE) if has_early else None, (head, FAR))
        if has_early:
            part_copy(head + 2, CORE).start()

            @pl.when(head + 3 < heads)
            def _():
                send_queries(head + 3, CORE)
        if has_late:
            final_copy(head - 1).wait_recv()
        step((head + 2, OWN) if has_early else None, (head - 1, CORE) if has_late else None)
        if has_late:
            term_copy(head - 1, CORE).start()
            finish_keys(head - 1)
        if has_early:
            send_lead(head + 2)

    begin(0)
    on_far(lambda: send_queries(1, FAR))
    begin(1)
    one_head(0, False, True)

    def middle(head, carry):
        one_head(head, True, True)

        @pl.when(head >= 2)
        def _():
            finish_queries(head - 2)

        return carry

    lax.fori_loop(1, heads - 2, middle, 0)

    def ending(head, carry):
        wait_queries(head, FAR)
        step((head, FAR), None)

        @pl.when(has_far)
        def _():
            part_copy(head, FAR).start()

            @pl.when(head == heads - 2)
            def _():
                term_copy(head - 1, FAR).start()

        settle_far(head)
        step(None, (head, FAR))
        on_far(lambda: term_copy(head, FAR).start())
        settle_own(head - 1)
        step(None, (head - 1, OWN))
        final_copy(head - 1).wait_recv()
        step(None, (head - 1, CORE))
        term_copy(head - 1, CORE).start()
        finish_keys(head - 1)
        finish_queries(head - 2)
        return carry

    lax.fori_loop(heads - 2, heads, ending, 0)
    end = heads - 1
    settle_own(end)
    step(None, (end, OWN))
    finish_queries(end - 1)
    final_copy(end).wait_recv()
    step(None, (end, CORE))
    term_copy(end, CORE).start()
    finish_keys(end)
    finish_queries(end)

    def drain(head, carry):
        def wait(role):
            q_copy(head, role).wait_send()
            g_copy(head, role).wait_send()
            part_copy(head, role).wait_send()
            term_copy(head, role).wait_send()
            if role == FAR:
                lead_copy(head).wait_send()
        each_partner(wait)
        final_copy(head).wait_send()
        for which in range(3):
            out_copy(head, which).wait()
        return carry

    lax.fori_loop(0, heads, drain, 0)


def place_kernel(*refs):
    sources, targets, (held, in_sem, out_sem) = refs[:3], refs[3:6], refs[6:]
    size = held.shape[1] // PIECES
    pieces = []
    for which in range(3):
        for piece in range(PIECES):
            part = pl.ds(piece * size, size)
            pieces.append((
                pltpu.make_async_copy(
                    sources[which].at[part], held.at[which, part], in_sem.at[which, piece]
                ),
                pltpu.make_async_copy(
                    held.at[which, part], targets[which].at[part], out_sem.at[which, piece]
                ),
            ))
    for copy_in, _ in pieces:
        copy_in.start()
    for copy_in, copy_out in pieces:
        copy_in.wait()
        copy_out.start()
    for _, copy_out in pieces:
        copy_out.wait()


def per_device(queries, keys_in, values, grad_out, clip_ids):
    row_tok, width = queries.shape
    heads = width // HEAD_DIM
    shape = jax.ShapeDtypeStruct((row_tok, width), LOW)
    anywhere = pl.BlockSpec(memory_space=pl.ANY)
    wide = jnp.float32
    dma = pltpu.SemaphoreType.DMA
    grads = pl.pallas_call(
        attention_kernel,
        out_shape=(shape, shape, shape),
        in_specs=[pl.BlockSpec(memory_space=pltpu.SMEM)] + [anywhere] * 4,
        out_specs=(anywhere, anywhere, anywhere),
        scratch_shapes=[
            pltpu.VMEM((3, heads, row_tok, HEAD_DIM), LOW),
            pltpu.VMEM((3, heads, row_tok, HEAD_DIM), LOW),
            pltpu.VMEM((heads, row_tok, HEAD_DIM), LOW),
            pltpu.VMEM((heads, row_tok, HEAD_DIM), LOW),
            pltpu.VMEM((row_tok, row_tok), wide),
            *(pltpu.VMEM((slots, row_tok, row_tok), wide) for slots in SLOTS),
            *(pltpu.VMEM((slots, row_tok, row_tok), LOW) for slots in SLOTS),
            pltpu.VMEM((row_tok, row_tok), LOW),
            pltpu.VMEM((row_tok, row_tok), LOW),
            *[pltpu.VMEM((heads, 1, row_tok), wide)] * 3,
            pltpu.VMEM((3, heads, 2, row_tok), wide),
            pltpu.VMEM((2, heads, 2, row_tok), wide),
            *[pltpu.VMEM((heads, 2, row_tok), wide)] * 5,
            pltpu.VMEM((2, heads, HEAD_DIM, row_tok), LOW),
            pltpu.VMEM((2, heads, HEAD_DIM, row_tok), LOW),
            pltpu.VMEM((heads, HEAD_DIM, row_tok), wide),
            pltpu.VMEM((2, 2, row_tok, HEAD_DIM), wide),
            pltpu.VMEM((3, heads, row_tok, HEAD_DIM), LOW),
            dma((4, heads)),
            dma((2, 2, heads)), dma((2, 2, heads)),
            dma((2, heads)), dma((2, heads)),
            dma((heads,)), dma((heads,)),
            dma((heads,)), dma((heads,)),
            dma((2, heads)), dma((2, heads)),
            dma((3, heads)),
        ],
        compiler_params=pltpu.CompilerParams(
            collective_id=0, has_side_effects=True, vmem_limit_bytes=58 * 1024 * 1024
        ),
    )(clip_ids, queries, keys_in, values, grad_out)
    return pl.pallas_call(
        place_kernel,
        out_shape=(shape, shape, shape),
        in_specs=[anywhere] * 3,
        out_specs=(anywhere, anywhere, anywhere),
        scratch_shapes=[
            pltpu.VMEM((3, row_tok, width), LOW), dma((3, PIECES)), dma((3, PIECES)),
        ],
        compiler_params=pltpu.CompilerParams(vmem_limit_bytes=58 * 1024 * 1024),
    )(*grads)


def solution(mesh):
    tokens = P(("groups", "ctx", "rep"), "head")
    return jax.shard_map(
        per_device,
        mesh=mesh,
        in_specs=(tokens, tokens, tokens, tokens, P("groups")),
        out_specs=(tokens, tokens, tokens),
        check_vma=False,
    )
```
